512 devices in a mesh: pair: 16 (over z, core), virt: 32 (over x, y).
Axes of the slice: x: 4, y: 8, z: 8, core: 2. Of those that a mesh axis runs over, the one named last changes fastest.
Arguments:
- amplitudes: bfloat16 [1024, 512, 512], P('pair', 'virt')
- integrals: bfloat16 [8, 512, 512, 512], P(None, 'pair', 'virt')
- pair_occ: int32 [1024, 2], P('virt'), may hold values from 0 to 119, as said below
- occ_irrep: int32 [120], replicated, may hold values from 0 to 7, as said below
- virt_irrep: int32 [512], replicated, may hold values from 0 to 7, as said below
- occ_energy: float32 [120], replicated, may hold values from -3 to -0.5
- virt_energy: float32 [512], replicated, may hold values from 0.3 to 4
Outputs:
- update: float32 [1024, 8, 512], P('virt', None, 'pair')
The draws below stay inside these ranges and needn't reach their ends.
Inputs may be any that keep to these rules, and one draw needn't show every extreme that they name: `pair_occ`: each row holds i < j, and rows are distinct. `occ_irrep`: labels of the D2h irreps; every label occurs. `virt_irrep`: labels of the D2h irreps; every label occurs.
All inputs are finite; a program needn't handle non-finite values.
Results may differ from the reference program's by a relative error of at most 0.0003.
Values may be sent and summed in bfloat16 or wider, within the bound.
A program may use at most 128 MiB of HBM per device.

```python
import jax
import jax.numpy as jnp
from jax import lax

NV = 512
NO = 120
WINDOW = 8
NPAIR = 1024


def irrep_labels(key, salt, count):
    labels = jax.random.randint(jax.random.fold_in(key, salt), (count,), 0, 8).astype(jnp.int32)
    order = jax.random.permutation(jax.random.fold_in(key, salt + 1), 8).astype(jnp.int32)
    padded = jnp.concatenate([order, jnp.zeros((count - 8,), jnp.int32)])
    position = jnp.arange(count, dtype=jnp.int32)
    return jnp.where(position < 8, padded, labels)


def draw_occ_irrep(key, part):
    return irrep_labels(key, 101, NO)


def draw_virt_irrep(key, part):
    return irrep_labels(key, 201, NV)


def draw_pair_occ(key, part):
    total_pairs = NO * (NO - 1) // 2
    anchor = NO - 2
    pair_key = jax.random.fold_in(key, 301)
    shuffled = jax.random.permutation(pair_key, total_pairs - 1)[:NPAIR - 1]
    shuffled = jnp.where(shuffled >= anchor, shuffled + 1, shuffled)
    chosen = jnp.concatenate([jnp.array([anchor], jnp.int32), shuffled.astype(jnp.int32)])
    orbital = jnp.arange(NO, dtype=jnp.int32)
    starts = orbital * (2 * NO - orbital - 1) // 2
    first = jnp.sum((starts[None, :] <= chosen[:, None]).astype(jnp.int32), axis=1) - 1
    first_start = jnp.sum(jnp.where(orbital[None, :] == first[:, None], starts[None, :], 0), axis=1)
    second = chosen - first_start + first + 1
    return jnp.stack([first, second], axis=1).astype(jnp.int32)


def base_values(key, shape):
    return jnp.clip(jax.random.normal(key, shape, jnp.float32), -6.0, 6.0)


def draw_amplitudes(key, part):
    occ_labels = draw_occ_irrep(key, part)
    virt_labels = draw_virt_irrep(key, part)
    pairs = draw_pair_occ(key, part)
    pair_sym = jnp.bitwise_xor(occ_labels[pairs[:, 0]], occ_labels[pairs[:, 1]])
    values = base_values(jax.random.fold_in(key, 401), (NPAIR, NV, NV))
    cd_sym = jnp.bitwise_xor(virt_labels[:, None], virt_labels[None, :])
    allowed = jnp.bitwise_xor(pair_sym[:, None, None], cd_sym[None, :, :]) == 0
    return jnp.where(allowed, values, 0.0).astype(jnp.bfloat16)


def draw_integrals(key, part):
    virt_labels = draw_virt_irrep(key, part)
    values = base_values(jax.random.fold_in(key, 501), (WINDOW, NV, NV, NV)) * (NV * NV / 8.0) ** (-0.5)
    ab_sym = jnp.bitwise_xor(virt_labels[:WINDOW, None], virt_labels[None, :])
    cd_sym = jnp.bitwise_xor(virt_labels[:, None], virt_labels[None, :])
    allowed = jnp.bitwise_xor(ab_sym[:, :, None, None], cd_sym[None, None, :, :]) == 0
    return jnp.where(allowed, values, 0.0).astype(jnp.bfloat16)


def setup_inputs(seed: int = 0) -> dict:
    streams_of = jax.random.split(jax.random.key(seed), 8)
    amplitudes = draw_amplitudes(jax.random.fold_in(streams_of[7], 71), 0)
    integrals = draw_integrals(jax.random.fold_in(streams_of[7], 71), 0)
    pair_occ = draw_pair_occ(jax.random.fold_in(streams_of[7], 71), 0)
    occ_irrep = draw_occ_irrep(jax.random.fold_in(streams_of[7], 71), 0)
    virt_irrep = draw_virt_irrep(jax.random.fold_in(streams_of[7], 71), 0)
    occ_energy = jnp.clip(jax.random.uniform(streams_of[5], (NO,), jnp.float32, -3.0, -0.5), -3.0, -0.5)
    virt_energy = jnp.clip(jax.random.uniform(streams_of[6], (NV,), jnp.float32, 0.3, 4.0), 0.3, 4.0)
    return dict(amplitudes=amplitudes, integrals=integrals, pair_occ=pair_occ, occ_irrep=occ_irrep, virt_irrep=virt_irrep, occ_energy=occ_energy, virt_energy=virt_energy)


def reference(amplitudes, integrals, pair_occ, occ_irrep, virt_irrep, occ_energy, virt_energy):
    pair_count = amplitudes.shape[0]
    flattened = amplitudes.reshape(pair_count, NV * NV)

    def one_window_row(block):
        return jnp.dot(flattened, block.reshape(NV, NV * NV).T, preferred_element_type=jnp.float32)

    ladder = jnp.transpose(lax.map(one_window_row, integrals), (1, 0, 2))
    first_occ = pair_occ[:, 0]
    second_occ = pair_occ[:, 1]
    pair_sym = jnp.bitwise_xor(occ_irrep[first_occ], occ_irrep[second_occ])
    window_sym = virt_irrep[:WINDOW]
    total_sym = jnp.bitwise_xor(pair_sym[:, None, None], jnp.bitwise_xor(window_sym[None, :, None], virt_irrep[None, None, :]))
    allowed = total_sym == 0
    denom = (occ_energy[first_occ] + occ_energy[second_occ])[:, None, None] - virt_energy[:WINDOW][None, :, None] - virt_energy[None, None, :]
    return jnp.where(allowed, ladder / denom, jnp.zeros_like(ladder))
```

```python
import functools

import jax
import jax.numpy as jnp
from jax import lax
from jax.experimental import pallas as pl
from jax.experimental.pallas import tpu as pltpu
from jax.sharding import PartitionSpec as P

MESH = pl.DeviceIdType.MESH
F32 = jnp.float32
BF16 = jnp.bfloat16

IRREPS = 8
LANES = 128
ROWS = 96
CLASS_ROW = ROWS - 1
OUT_SLOTS = 64
CORES = 2


def iota(shape, dim):
    return lax.broadcasted_iota(jnp.int32, shape, dim)


def mm(a, b):
    return lax.dot_general(a, b, (((1,), (0,)), ((), ())), preferred_element_type=F32)


def split3(x):
    hi = x.astype(BF16)
    rest = x - hi.astype(F32)
    mid = rest.astype(BF16)
    return hi, mid, (rest - mid.astype(F32)).astype(BF16)


def select_dot(sel, x):
    n = x.shape[1]
    both = mm(sel, jnp.concatenate(split3(x), axis=1))
    return (both[:, 2 * n :] + both[:, n : 2 * n]) + both[:, :n]


def fold_kernel(
    chips,
    virts,
    t_hbm,
    v_hbm,
    po_ref,
    oi_ref,
    vi_ref,
    oe_ref,
    ve_ref,
    out_ref,
    t_buf,
    v_buf,
    small,
    slot_sel,
    group_sel,
    t_folded,
    t_seen,
    v_folded,
    v_mat,
    cls_ref,
    fold_sel,
    own,
    sib,
    stage,
    recv,
    local_sem,
    ring_send,
    ring_recv,
    sib_send,
    sib_recv,
    piece_send,
    piece_recv,
):
    pairs, depth, width = t_buf.shape
    window, bwidth = v_buf.shape[0], v_buf.shape[1]
    abs_ = window * bwidth
    half_c = depth // 2
    chunk = half_c // 2

    pair = lax.axis_index("pair")
    virt = lax.axis_index("virt")
    z = lax.div(pair, CORES)
    core = lax.rem(pair, CORES)
    up = lax.rem(z + 1, chips) * CORES + core
    down = lax.rem(z + chips - 1, chips) * CORES + core
    other = z * CORES + (1 - core)

    t_copy = pltpu.make_async_copy(t_hbm, t_buf, local_sem.at[0])
    v_copy = pltpu.make_async_copy(v_hbm, v_buf, local_sem.at[1])
    t_copy.start()
    v_copy.start()

    barrier = pltpu.get_barrier_semaphore()
    for q in (up, down, other):
        pl.semaphore_signal(barrier, inc=1, device_id={"pair": q}, device_id_type=MESH)

    @pl.loop(1, virts)
    def _(k):
        w = lax.rem(virt + k, virts)
        pl.semaphore_signal(barrier, inc=1, device_id={"virt": w}, device_id_type=MESH)

    for blocks in (own, sib):
        blocks[:, :, ROWS:, :] = jnp.zeros((chips, half_c, LANES - ROWS, LANES), BF16)

    vi = vi_ref[...].astype(F32)
    ve = ve_ref[...]
    lane_d = iota((width, width), 1)
    sub_d = iota((width, width), 0)
    irr_col = jnp.sum(jnp.where(lane_d == sub_d, vi, 0.0), axis=1, keepdims=True)
    lane_g = iota((width, LANES), 1)
    hot = irr_col.astype(jnp.int32) == lane_g
    hot_f = jnp.where(hot, 1.0, 0.0)
    earlier = jnp.where(lane_d < sub_d, 1.0, 0.0).astype(BF16)
    counts = mm(earlier, hot_f.astype(BF16))
    slot = jnp.sum(jnp.where(hot, counts, 0.0), axis=1, keepdims=True)
    slot_sel[...] = jnp.where(slot.astype(jnp.int32) == lane_g, 1.0, 0.0).astype(BF16)
    group_sel[...] = hot_f.astype(BF16)

    lane_c = iota((depth, width), 1)
    sub_c = iota((depth, width), 0)
    irr_c = jnp.sum(jnp.where(lane_c == virt * depth + sub_c, vi, 0.0), axis=1, keepdims=True)
    lane_s = iota((depth, LANES), 1)
    seen_class = jnp.where(
        lane_s < IRREPS, jnp.bitwise_xor(irr_c.astype(jnp.int32), lane_s), 0
    ).astype(F32)

    lane_ab = iota((abs_, width), 1)
    sub_ab = iota((abs_, width), 0)
    sub_a = lax.div(sub_ab, bwidth)
    hit_a = lane_ab == sub_a
    hit_b = lane_ab == pair * bwidth + (sub_ab - sub_a * bwidth)
    irr_a = jnp.sum(jnp.where(hit_a, vi, 0.0), axis=1, keepdims=True)
    irr_b = jnp.sum(jnp.where(hit_b, vi, 0.0), axis=1, keepdims=True)
    energy_a = jnp.sum(jnp.where(hit_a, ve, 0.0), axis=1, keepdims=True)
    energy_b = jnp.sum(jnp.where(hit_b, ve, 0.0), axis=1, keepdims=True)
    cls = jnp.bitwise_xor(irr_a.astype(jnp.int32), irr_b.astype(jnp.int32))
    lane_k = iota((abs_, LANES), 1)
    hot_ab = cls == lane_k
    hot_ab_f = jnp.where(hot_ab, 1.0, 0.0)
    before = jnp.where(iota((abs_, abs_), 1) < iota((abs_, abs_), 0), 1.0, 0.0).astype(BF16)
    ranks = jnp.where(hot_ab, mm(before, hot_ab_f.astype(BF16)), 0.0)
    rank = jnp.sum(ranks, axis=1, keepdims=True).astype(jnp.int32)
    unfold_f = jnp.where(rank == lane_k, 1.0, 0.0)
    unfold = unfold_f.astype(BF16)[:, :OUT_SLOTS]
    fold_sel[...] = jnp.transpose(unfold_f)[:OUT_SLOTS, :].astype(BF16)
    cls_ref[...] = jnp.broadcast_to(cls.astype(F32), (abs_, LANES))

    t_copy.wait()
    rows = pairs * depth
    t_rows = t_buf[...].reshape(rows, width)
    t_folded[...] = mm(t_rows, slot_sel[...])
    live = jnp.where(t_rows.astype(F32) != 0.0, 1.0, 0.0).astype(BF16)
    seen = mm(live, group_sel[...]).reshape(pairs, depth, LANES)
    t_seen[...] = jnp.where(seen > 0.0, seen_class[None], 0.0).reshape(rows, LANES)
    pair_cls = t_seen[pl.ds(0, pairs, stride=depth), :]
    for c in range(1, depth):
        pair_cls = jnp.maximum(pair_cls, t_seen[pl.ds(c, pairs, stride=depth), :])
    pair_cls = jnp.max(pair_cls, axis=1, keepdims=True)

    def fold_block(c2):
        x = jnp.concatenate(
            [
                t_folded[pl.ds(c2, pairs, stride=depth), :],
                t_folded[pl.ds(c2 + half_c, pairs, stride=depth), :],
            ],
            axis=0,
        )
        if c2 == 0:
            label = jnp.concatenate([pair_cls, pair_cls], axis=0)
            x = jnp.where(iota(x.shape, 1) == CLASS_ROW, label, x)
        own[0, c2, :ROWS, :] = jnp.transpose(x)[:ROWS, :].astype(BF16)

    def part(blocks, delta, ch):
        return blocks.at[delta, pl.ds(ch * chunk, chunk), pl.ds(0, ROWS), :]

    def ring_copy(way, d, ch):
        src, dst = d - 1, d
        if way == 0:
            src, dst = (chips - src) % chips, (chips - dst) % chips
        return pltpu.make_async_remote_copy(
            src_ref=part(own, src, ch),
            dst_ref=part(own, dst, ch),
            send_sem=ring_send.at[way, d - 1, ch],
            recv_sem=ring_recv.at[way, d - 1, ch],
            device_id={"pair": up if way == 0 else down},
            device_id_type=MESH,
        )

    def sib_copy(delta, ch):
        return pltpu.make_async_remote_copy(
            src_ref=part(own, delta, ch),
            dst_ref=part(sib, delta, ch),
            send_sem=sib_send.at[delta, ch],
            recv_sem=sib_recv.at[delta, ch],
            device_id={"pair": other},
            device_id_type=MESH,
        )

    far = chips // 2

    def travels(way, d, ch):
        return d < far or (d == far and ch == way)

    for c2 in range(chunk):
        fold_block(c2)
    pl.semaphore_wait(barrier, virts - 1 + 3)
    ring_copy(0, 1, 0).start()
    ring_copy(1, 1, 0).start()
    sib_copy(0, 0).start()
    for c2 in range(chunk, half_c):
        fold_block(c2)
    ring_copy(0, 1, 1).start()
    ring_copy(1, 1, 1).start()
    sib_copy(0, 1).start()

    v_copy.wait()

    @pl.loop(0, window)
    def _(a):
        v_folded[...] = mm(v_buf[a].reshape(bwidth * depth, width), slot_sel[...])
        dst = pl.ds(pl.multiple_of(a * bwidth, bwidth), bwidth)
        for c in range(depth):
            x = v_folded[pl.ds(c, bwidth, stride=depth), :].astype(BF16)
            c2 = c % half_c
            v_mat[c // half_c, dst, c2 * LANES : (c2 + 1) * LANES] = x

    def piece_copy(owner):
        r = lax.rem(virt - owner + virts, virts) - 1
        return pltpu.make_async_remote_copy(
            src_ref=stage.at[owner],
            dst_ref=recv.at[r],
            send_sem=piece_send,
            recv_sem=piece_recv,
            device_id={"virt": owner},
            device_id_type=MESH,
        )

    lane = iota((1, LANES), 1)
    low = lane < pairs
    quarter = lax.div(lane, LANES // 4)

    def contract(delta):
        k = half_c * LANES
        block = jnp.concatenate(
            [own[delta].reshape(k, LANES), sib[delta].reshape(k, LANES)], axis=1
        )
        r0 = mm(v_mat[0], block)
        r1 = mm(v_mat[1], block)
        keep = jnp.where(low, r0[:, :LANES], r1[:, LANES:])
        move = jnp.where(low, r0[:, LANES:], r1[:, :LANES])
        full = keep + pltpu.roll(move, LANES // 2, axis=1)
        tail = ROWS - 16
        row_own = own[delta, 0, tail:ROWS, :].astype(F32)[15:16, :]
        row_sib = sib[delta, 0, tail:ROWS, :].astype(F32)[15:16, :]
        row = jnp.where(low, row_own, row_sib)
        full = jnp.where(cls_ref[...] == row, full, 0.0)
        folded = select_dot(fold_sel[...], full)
        far_z = lax.rem(z + delta, chips)
        per = OUT_SLOTS // 4
        for u in range(4):
            piece = jnp.zeros((per, LANES), F32)
            for q in range(4):
                x = folded[q * per : (q + 1) * per, :]
                shift = ((q - u) % 4) * (LANES // 4)
                if shift:
                    x = pltpu.roll(x, shift, axis=1)
                piece = jnp.where(quarter == q, x, piece)
            block_pair = far_z * CORES + (core if u < 2 else 1 - core)
            owner = block_pair * 2 + u % 2
            stage[owner] = piece

            @pl.when(owner != virt)
            def _():
                piece_copy(owner).start()

    def ready(delta):
        for ch in range(2):
            sib_copy(delta, ch).wait_recv()
        contract(delta)

    def arrive(d, ch):
        for way in range(2):
            if travels(way, d, ch):
                ring_copy(way, d, ch).wait_recv()
                if travels(way, d + 1, ch):
                    ring_copy(way, d + 1, ch).start()
                sib_copy((chips - d) % chips if way == 0 else d, ch).start()

    arrive(1, 0)
    ready(0)
    arrive(1, 1)
    for d in range(2, far):
        arrive(d, 0)
        ready(chips - (d - 1))
        arrive(d, 1)
        ready(d - 1)
    if far > 1:
        ready(chips - (far - 1))
    arrive(far, 0)
    arrive(far, 1)
    if far > 1:
        ready(far - 1)
    ready(far)

    pltpu.make_async_copy(recv, recv, piece_recv).wait()
    total = stage[virt]
    for r in range(virts - 1):
        total = total + recv[r]
    shifted = [total] + [pltpu.roll(total, LANES - q * (LANES // 4), axis=1) for q in (1, 2, 3)]
    ladder = select_dot(unfold, jnp.concatenate(shifted, axis=0))

    small[...] = jnp.zeros_like(small)
    small[0:1, : oi_ref.shape[1]] = oi_ref[...].astype(F32)
    small[1:2, : oe_ref.shape[1]] = oe_ref[...]
    small[2:4, : po_ref.shape[1]] = po_ref[...].astype(F32)
    orb_irr = jnp.transpose(jnp.broadcast_to(small[0:1, :], (LANES, LANES)))
    orb_energy = jnp.transpose(jnp.broadcast_to(small[1:2, :], (LANES, LANES)))
    orb = iota((LANES, LANES), 0)
    hit_i = small[2:3, :].astype(jnp.int32) == orb
    hit_j = small[3:4, :].astype(jnp.int32) == orb
    irr_i = jnp.sum(jnp.where(hit_i, orb_irr, 0.0), axis=0, keepdims=True)
    irr_j = jnp.sum(jnp.where(hit_j, orb_irr, 0.0), axis=0, keepdims=True)
    energy_i = jnp.sum(jnp.where(hit_i, orb_energy, 0.0), axis=0, keepdims=True)
    energy_j = jnp.sum(jnp.where(hit_j, orb_energy, 0.0), axis=0, keepdims=True)
    pair_sym = jnp.bitwise_xor(irr_i.astype(jnp.int32), irr_j.astype(jnp.int32)).astype(F32)
    denom = ((energy_i + energy_j) - energy_a) - energy_b
    update = jnp.where(cls_ref[...] == pair_sym, ladder / denom, 0.0)
    out_ref[...] = jnp.transpose(update)[: out_ref.shape[0], :]

    for way in range(2):
        for d in range(1, far + 1):
            for ch in range(2):
                if travels(way, d, ch):
                    ring_copy(way, d, ch).wait_send()
    for delta in range(chips):
        for ch in range(2):
            sib_copy(delta, ch).wait_send()
    pltpu.make_async_copy(recv, recv, piece_send).wait()


def folded(mesh, amplitudes, integrals, pair_occ, occ_irrep, virt_irrep, occ_energy, virt_energy):
    chips, virts = mesh.shape["pair"] // CORES, mesh.shape["virt"]
    pairs, depth, width = amplitudes.shape
    window, bwidth = integrals.shape[:2]
    abs_ = window * bwidth
    owned = pair_occ.shape[0]
    half_c = depth // 2
    per = OUT_SLOTS // 4
    vmem = pl.BlockSpec(memory_space=pltpu.VMEM)
    hbm = pl.BlockSpec(memory_space=pl.ANY)
    dma = pltpu.SemaphoreType.DMA
    out = pl.pallas_call(
        functools.partial(fold_kernel, chips, virts),
        out_shape=jax.ShapeDtypeStruct((owned, abs_), F32),
        in_specs=[hbm, hbm] + [vmem] * 5,
        out_specs=vmem,
        scratch_shapes=[
            pltpu.VMEM(amplitudes.shape, BF16),
            pltpu.VMEM(integrals.shape, BF16),
            pltpu.VMEM((8, LANES), F32),
            pltpu.VMEM((width, LANES), BF16),
            pltpu.VMEM((width, LANES), BF16),
            pltpu.VMEM((pairs * depth, LANES), F32),
            pltpu.VMEM((pairs * depth, LANES), F32),
            pltpu.VMEM((bwidth * depth, LANES), F32),
            pltpu.VMEM((2, abs_, half_c * LANES), BF16),
            pltpu.VMEM((abs_, LANES), F32),
            pltpu.VMEM((OUT_SLOTS, abs_), BF16),
            pltpu.VMEM((chips, half_c, LANES, LANES), BF16),
            pltpu.VMEM((chips, half_c, LANES, LANES), BF16),
            pltpu.VMEM((virts, per, LANES), F32),
            pltpu.VMEM((virts - 1, per, LANES), F32),
            dma((2,)),
            dma((2, chips // 2, 2)),
            dma((2, chips // 2, 2)),
            dma((chips, 2)),
            dma((chips, 2)),
            dma,
            dma,
        ],
        compiler_params=pltpu.CompilerParams(collective_id=0, has_side_effects=True),
        name="ladder_fold",
    )(
        amplitudes,
        integrals,
        pair_occ.T,
        occ_irrep[None, :],
        virt_irrep[None, :],
        occ_energy[None, :],
        virt_energy[None, :],
    )
    return out.reshape(owned, window, bwidth)


def fits(window, bwidth, virt_irrep):
    groups = jnp.arange(IRREPS, dtype=jnp.int32)
    hot = virt_irrep[None, :] == groups[:, None]
    sizes = jnp.sum(hot.astype(jnp.int32), axis=1)
    label = jnp.bitwise_xor(virt_irrep[:window, None], virt_irrep[None, :])
    label = label.reshape(window, -1, bwidth)
    members = jnp.sum((label[None] == groups[:, None, None, None]).astype(jnp.int32), axis=(1, 3))
    return jnp.logical_and(jnp.max(sizes) <= CLASS_ROW, jnp.max(members) <= OUT_SLOTS)


def table_lookup(indices, table, zero_value):
    orbital = jnp.arange(table.shape[0], dtype=jnp.int32)
    hits = indices[:, None] == orbital[None, :]
    return jnp.sum(jnp.where(hits, table[None, :], zero_value), axis=1)


def general(amplitudes, integrals, pair_occ, occ_irrep, virt_irrep, occ_energy, virt_energy):
    window_size, local_width, local_depth, full_width = integrals.shape
    integral_matrix = integrals.reshape(window_size * local_width, local_depth * full_width)
    owned_rows = pair_occ.shape[0]
    block_rows = lax.all_gather(amplitudes, "pair", axis=0, tiled=True)
    flattened = block_rows.reshape(block_rows.shape[0], local_depth * full_width)
    partial_value = lax.dot_general(
        flattened, integral_matrix, (((1,), (1,)), ((), ())), preferred_element_type=jnp.float32
    )
    summed = lax.psum(partial_value, "virt")
    ladder = lax.dynamic_slice_in_dim(summed, lax.axis_index("virt") * owned_rows, owned_rows, 0)
    ladder = ladder.reshape(owned_rows, window_size, local_width)
    b_offset = lax.axis_index("pair") * local_width
    local_sym = lax.dynamic_slice_in_dim(virt_irrep, b_offset, local_width, 0)
    local_energy = lax.dynamic_slice_in_dim(virt_energy, b_offset, local_width, 0)
    first_occ = pair_occ[:, 0]
    second_occ = pair_occ[:, 1]
    pair_sym = jnp.bitwise_xor(
        table_lookup(first_occ, occ_irrep, 0), table_lookup(second_occ, occ_irrep, 0)
    )
    pair_energy = table_lookup(first_occ, occ_energy, 0.0) + table_lookup(
        second_occ, occ_energy, 0.0
    )
    window_sym = virt_irrep[:window_size]
    total_sym = jnp.bitwise_xor(
        pair_sym[:, None, None],
        jnp.bitwise_xor(window_sym[None, :, None], local_sym[None, None, :]),
    )
    allowed = total_sym == 0
    denom = (
        pair_energy[:, None, None]
        - virt_energy[:window_size][None, :, None]
        - local_energy[None, None, :]
    )
    return jnp.where(allowed, ladder / denom, jnp.zeros_like(ladder))


def solution(mesh):
    def local(*args):
        window, bwidth = args[1].shape[:2]
        return lax.cond(
            fits(window, bwidth, args[4]), functools.partial(folded, mesh), general, *args
        )

    return jax.shard_map(
        local,
        mesh=mesh,
        in_specs=(
            P("pair", "virt", None),
            P(None, "pair", "virt", None),
            P("virt", None),
            P(),
            P(),
            P(),
            P(),
        ),
        out_specs=P("virt", None, "pair"),
        check_vma=False,
    )
```

```python
import functools

import jax
import jax.numpy as jnp
from jax import lax
from jax.experimental import pallas as pl
from jax.experimental.pallas import tpu as pltpu
from jax.sharding import PartitionSpec as P

MESH = pl.DeviceIdType.MESH
F32 = jnp.float32
BF16 = jnp.bfloat16

IRREPS = 8
LANES = 128
ROWS = 96
CLASS_ROW = ROWS - 1
OUT_SLOTS = 64
CORES = 2


def iota(shape, dim):
    return lax.broadcasted_iota(jnp.int32, shape, dim)


def mm(a, b):
    return lax.dot_general(a, b, (((1,), (0,)), ((), ())), preferred_element_type=F32)


def split3(x):
    hi = x.astype(BF16)
    rest = x - hi.astype(F32)
    mid = rest.astype(BF16)
    return hi, mid, (rest - mid.astype(F32)).astype(BF16)


def select_dot(sel, x):
    n = x.shape[1]
    both = mm(sel, jnp.concatenate(split3(x), axis=1))
    return (both[:, 2 * n :] + both[:, n : 2 * n]) + both[:, :n]


def fold_kernel(
    chips,
    virts,
    t_hbm,
    v_hbm,
    po_ref,
    oi_ref,
    vi_ref,
    oe_ref,
    ve_ref,
    out_ref,
    t_buf,
    v_buf,
    small,
    slot_sel,
    group_sel,
    t_folded,
    t_seen,
    v_folded,
    v_mat,
    cls_ref,
    fold_sel,
    own,
    sib,
    stage,
    recv,
    local_sem,
    ring_send,
    ring_recv,
    sib_send,
    sib_recv,
    piece_send,
    piece_recv,
):
    pairs, depth, width = t_buf.shape
    window, bwidth = v_buf.shape[0], v_buf.shape[1]
    abs_ = window * bwidth
    half_c = depth // 2
    chunk = half_c // 2

    pair = lax.axis_index("pair")
    virt = lax.axis_index("virt")
    z = lax.div(pair, CORES)
    core = lax.rem(pair, CORES)
    up = lax.rem(z + 1, chips) * CORES + core
    down = lax.rem(z + chips - 1, chips) * CORES + core
    other = z * CORES + (1 - core)

    t_copy = pltpu.make_async_copy(t_hbm, t_buf, local_sem.at[0])
    v_copy = pltpu.make_async_copy(v_hbm, v_buf, local_sem.at[1])
    t_copy.start()
    v_copy.start()

    barrier = pltpu.get_barrier_semaphore()
    for q in (up, down, other):
        pl.semaphore_signal(barrier, inc=1, device_id={"pair": q}, device_id_type=MESH)

    @pl.loop(1, virts)
    def _(k):
        w = lax.rem(virt + k, virts)
        pl.semaphore_signal(barrier, inc=1, device_id={"virt": w}, device_id_type=MESH)

    for blocks in (own, sib):
        blocks[:, :, ROWS:, :] = jnp.zeros((chips, half_c, LANES - ROWS, LANES), BF16)

    vi = vi_ref[...].astype(F32)
    ve = ve_ref[...]
    lane_d = iota((width, width), 1)
    sub_d = iota((width, width), 0)
    irr_col = jnp.sum(jnp.where(lane_d == sub_d, vi, 0.0), axis=1, keepdims=True)
    lane_g = iota((width, LANES), 1)
    hot = irr_col.astype(jnp.int32) == lane_g
    hot_f = jnp.where(hot, 1.0, 0.0)
    earlier = jnp.where(lane_d < sub_d, 1.0, 0.0).astype(BF16)
    counts = mm(earlier, hot_f.astype(BF16))
    slot = jnp.sum(jnp.where(hot, counts, 0.0), axis=1, keepdims=True)
    slot_sel[...] = jnp.where(slot.astype(jnp.int32) == lane_g, 1.0, 0.0).astype(BF16)
    group_sel[...] = hot_f.astype(BF16)

    lane_c = iota((depth, width), 1)
    sub_c = iota((depth, width), 0)
    irr_c = jnp.sum(jnp.where(lane_c == virt * depth + sub_c, vi, 0.0), axis=1, keepdims=True)
    lane_s = iota((depth, LANES), 1)
    seen_class = jnp.where(
        lane_s < IRREPS, jnp.bitwise_xor(irr_c.astype(jnp.int32), lane_s), 0
    ).astype(F32)

    lane_ab = iota((abs_, width), 1)
    sub_ab = iota((abs_, width), 0)
    sub_a = lax.div(sub_ab, bwidth)
    hit_a = lane_ab == sub_a
    hit_b = lane_ab == pair * bwidth + (sub_ab - sub_a * bwidth)
    irr_a = jnp.sum(jnp.where(hit_a, vi, 0.0), axis=1, keepdims=True)
    irr_b = jnp.sum(jnp.where(hit_b, vi, 0.0), axis=1, keepdims=True)
    energy_a = jnp.sum(jnp.where(hit_a, ve, 0.0), axis=1, keepdims=True)
    energy_b = jnp.sum(jnp.where(hit_b, ve, 0.0), axis=1, keepdims=True)
    cls = jnp.bitwise_xor(irr_a.astype(jnp.int32), irr_b.astype(jnp.int32))
    lane_k = iota((abs_, LANES), 1)
    hot_ab = cls == lane_k
    hot_ab_f = jnp.where(hot_ab, 1.0, 0.0)
    before = jnp.where(iota((abs_, abs_), 1) < iota((abs_, abs_), 0), 1.0, 0.0).astype(BF16)
    ranks = jnp.where(hot_ab, mm(before, hot_ab_f.astype(BF16)), 0.0)
    rank = jnp.sum(ranks, axis=1, keepdims=True).astype(jnp.int32)
    unfold_f = jnp.where(rank == lane_k, 1.0, 0.0)
    unfold = unfold_f.astype(BF16)[:, :OUT_SLOTS]
    fold_sel[...] = jnp.transpose(unfold_f)[:OUT_SLOTS, :].astype(BF16)
    cls_ref[...] = jnp.broadcast_to(cls.astype(F32), (abs_, LANES))

    t_copy.wait()
    rows = pairs * depth
    t_rows = t_buf[...].reshape(rows, width)
    t_folded[...] = mm(t_rows, slot_sel[...])
    live = jnp.where(t_rows.astype(F32) != 0.0, 1.0, 0.0).astype(BF16)
    seen = mm(live, group_sel[...]).reshape(pairs, depth, LANES)
    t_seen[...] = jnp.where(seen > 0.0, seen_class[None], 0.0).reshape(rows, LANES)
    pair_cls = t_seen[pl.ds(0, pairs, stride=depth), :]
    for c in range(1, depth):
        pair_cls = jnp.maximum(pair_cls, t_seen[pl.ds(c, pairs, stride=depth), :])
    pair_cls = jnp.max(pair_cls, axis=1, keepdims=True)

    def fold_block(c2):
        x = jnp.concatenate(
            [
                t_folded[pl.ds(c2, pairs, stride=depth), :],
                t_folded[pl.ds(c2 + half_c, pairs, stride=depth), :],
            ],
            axis=0,
        )
        if c2 == 0:
            label = jnp.concatenate([pair_cls, pair_cls], axis=0)
            x = jnp.where(iota(x.shape, 1) == CLASS_ROW, label, x)
        own[0, c2, :ROWS, :] = jnp.transpose(x)[:ROWS, :].astype(BF16)

    def part(blocks, delta, ch):
        return blocks.at[delta, pl.ds(ch * chunk, chunk), pl.ds(0, ROWS), :]

    def ring_copy(way, d, ch):
        src, dst = d - 1, d
        if way == 0:
            src, dst = (chips - src) % chips, (chips - dst) % chips
        return pltpu.make_async_remote_copy(
            src_ref=part(own, src, ch),
            dst_ref=part(own, dst, ch),
            send_sem=ring_send.at[way, d - 1, ch],
            recv_sem=ring_recv.at[way, d - 1, ch],
            device_id={"pair": up if way == 0 else down},
            device_id_type=MESH,
        )

    def sib_copy(delta, ch):
        return pltpu.make_async_remote_copy(
            src_ref=part(own, delta, ch),
            dst_ref=part(sib, delta, ch),
            send_sem=sib_send.at[delta, ch],
            recv_sem=sib_recv.at[delta, ch],
            device_id={"pair": other},
            device_id_type=MESH,
        )

    far = chips // 2

    def travels(way, d, ch):
        return d < far or (d == far and ch == way)

    for c2 in range(chunk):
        fold_block(c2)
    pl.semaphore_wait(barrier, virts - 1 + 3)
    ring_copy(0, 1, 0).start()
    ring_copy(1, 1, 0).start()
    sib_copy(0, 0).start()
    for c2 in range(chunk, half_c):
        fold_block(c2)
    ring_copy(0, 1, 1).start()
    ring_copy(1, 1, 1).start()
    sib_copy(0, 1).start()

    v_copy.wait()

    @pl.loop(0, window)
    def _(a):
        v_folded[...] = mm(v_buf[a].reshape(bwidth * depth, width), slot_sel[...])
        dst = pl.ds(pl.multiple_of(a * bwidth, bwidth), bwidth)
        for c in range(depth):
            x = v_folded[pl.ds(c, bwidth, stride=depth), :].astype(BF16)
            c2 = c % half_c
            v_mat[c // half_c, dst, c2 * LANES : (c2 + 1) * LANES] = x

    def piece_copy(owner):
        r = lax.rem(virt - owner + virts, virts) - 1
        return pltpu.make_async_remote_copy(
            src_ref=stage.at[owner],
            dst_ref=recv.at[r],
            send_sem=piece_send,
            recv_sem=piece_recv,
            device_id={"virt": owner},
            device_id_type=MESH,
        )

    lane = iota((1, LANES), 1)
    low = lane < pairs
    quarter = lax.div(lane, LANES // 4)

    def contract(delta):
        k = half_c * LANES
        block = jnp.concatenate(
            [own[delta].reshape(k, LANES), sib[delta].reshape(k, LANES)], axis=1
        )
        r0 = mm(v_mat[0], block)
        r1 = mm(v_mat[1], block)
        keep = jnp.where(low, r0[:, :LANES], r1[:, LANES:])
        move = jnp.where(low, r0[:, LANES:], r1[:, :LANES])
        full = keep + pltpu.roll(move, LANES // 2, axis=1)
        tail = ROWS - 16
        row_own = own[delta, 0, tail:ROWS, :].astype(F32)[15:16, :]
        row_sib = sib[delta, 0, tail:ROWS, :].astype(F32)[15:16, :]
        row = jnp.where(low, row_own, row_sib)
        full = jnp.where(cls_ref[...] == row, full, 0.0)
        folded = select_dot(fold_sel[...], full)
        far_z = lax.rem(z + delta, chips)
        per = OUT_SLOTS // 4
        for u in range(4):
            piece = jnp.zeros((per, LANES), F32)
            for q in range(4):
                x = folded[q * per : (q + 1) * per, :]
                shift = ((q - u) % 4) * (LANES // 4)
                if shift:
                    x = pltpu.roll(x, shift, axis=1)
                piece = jnp.where(quarter == q, x, piece)
            block_pair = far_z * CORES + (core if u < 2 else 1 - core)
            owner = block_pair * 2 + u % 2
            stage[owner] = piece

            @pl.when(owner != virt)
            def _():
                piece_copy(owner).start()

    def ready(delta):
        for ch in range(2):
            sib_copy(delta, ch).wait_recv()
        contract(delta)

    def arrive(d, ch):
        for way in range(2):
            if travels(way, d, ch):
                ring_copy(way, d, ch).wait_recv()
                if travels(way, d + 1, ch):
                    ring_copy(way, d + 1, ch).start()
                sib_copy((chips - d) % chips if way == 0 else d, ch).start()

    arrive(1, 0)
    ready(0)
    arrive(1, 1)
    for d in range(2, far):
        arrive(d, 0)
        ready(chips - (d - 1))
        arrive(d, 1)
        ready(d - 1)
    if far > 1:
        ready(chips - (far - 1))
    arrive(far, 0)
    arrive(far, 1)
    if far > 1:
        ready(far - 1)
    ready(far)

    pltpu.make_async_copy(recv, recv, piece_recv).wait()
    total = stage[virt]
    for r in range(virts - 1):
        total = total + recv[r]
    shifted = [total] + [pltpu.roll(total, LANES - q * (LANES // 4), axis=1) for q in (1, 2, 3)]
    ladder = select_dot(unfold, jnp.concatenate(shifted, axis=0))

    small[...] = jnp.zeros_like(small)
    small[0:1, : oi_ref.shape[1]] = oi_ref[...].astype(F32)
    small[1:2, : oe_ref.shape[1]] = oe_ref[...]
    small[2:4, : po_ref.shape[1]] = po_ref[...].astype(F32)
    orb_irr = jnp.transpose(jnp.broadcast_to(small[0:1, :], (LANES, LANES)))
    orb_energy = jnp.transpose(jnp.broadcast_to(small[1:2, :], (LANES, LANES)))
    orb = iota((LANES, LANES), 0)
    hit_i = small[2:3, :].astype(jnp.int32) == orb
    hit_j = small[3:4, :].astype(jnp.int32) == orb
    irr_i = jnp.sum(jnp.where(hit_i, orb_irr, 0.0), axis=0, keepdims=True)
    irr_j = jnp.sum(jnp.where(hit_j, orb_irr, 0.0), axis=0, keepdims=True)
    energy_i = jnp.sum(jnp.where(hit_i, orb_energy, 0.0), axis=0, keepdims=True)
    energy_j = jnp.sum(jnp.where(hit_j, orb_energy, 0.0), axis=0, keepdims=True)
    pair_sym = jnp.bitwise_xor(irr_i.astype(jnp.int32), irr_j.astype(jnp.int32)).astype(F32)
    denom = ((energy_i + energy_j) - energy_a) - energy_b
    update = jnp.where(cls_ref[...] == pair_sym, ladder / denom, 0.0)
    update = jnp.transpose(update)[: out_ref.shape[0], :]
    for a in range(window):
        out_ref[:, a, :] = update[:, a * bwidth : (a + 1) * bwidth]

    for way in range(2):
        for d in range(1, far + 1):
            for ch in range(2):
                if travels(way, d, ch):
                    ring_copy(way, d, ch).wait_send()
    for delta in range(chips):
        for ch in range(2):
            sib_copy(delta, ch).wait_send()
    pltpu.make_async_copy(recv, recv, piece_send).wait()


def folded(mesh, amplitudes, integrals, pair_occ, occ_irrep, virt_irrep, occ_energy, virt_energy):
    chips, virts = mesh.shape["pair"] // CORES, mesh.shape["virt"]
    pairs, depth, width = amplitudes.shape
    window, bwidth = integrals.shape[:2]
    abs_ = window * bwidth
    owned = pair_occ.shape[0]
    half_c = depth // 2
    per = OUT_SLOTS // 4
    vmem = pl.BlockSpec(memory_space=pltpu.VMEM)
    hbm = pl.BlockSpec(memory_space=pl.ANY)
    dma = pltpu.SemaphoreType.DMA
    return pl.pallas_call(
        functools.partial(fold_kernel, chips, virts),
        out_shape=jax.ShapeDtypeStruct((owned, window, bwidth), F32),
        in_specs=[hbm, hbm] + [vmem] * 5,
        out_specs=vmem,
        scratch_shapes=[
            pltpu.VMEM(amplitudes.shape, BF16),
            pltpu.VMEM(integrals.shape, BF16),
            pltpu.VMEM((8, LANES), F32),
            pltpu.VMEM((width, LANES), BF16),
            pltpu.VMEM((width, LANES), BF16),
            pltpu.VMEM((pairs * depth, LANES), F32),
            pltpu.VMEM((pairs * depth, LANES), F32),
            pltpu.VMEM((bwidth * depth, LANES), F32),
            pltpu.VMEM((2, abs_, half_c * LANES), BF16),
            pltpu.VMEM((abs_, LANES), F32),
            pltpu.VMEM((OUT_SLOTS, abs_), BF16),
            pltpu.VMEM((chips, half_c, LANES, LANES), BF16),
            pltpu.VMEM((chips, half_c, LANES, LANES), BF16),
            pltpu.VMEM((virts, per, LANES), F32),
            pltpu.VMEM((virts - 1, per, LANES), F32),
            dma((2,)),
            dma((2, chips // 2, 2)),
            dma((2, chips // 2, 2)),
            dma((chips, 2)),
            dma((chips, 2)),
            dma,
            dma,
        ],
        compiler_params=pltpu.CompilerParams(collective_id=0, has_side_effects=True),
        name="ladder_fold",
    )(
        amplitudes,
        integrals,
        pair_occ.T,
        occ_irrep[None, :],
        virt_irrep[None, :],
        occ_energy[None, :],
        virt_energy[None, :],
    )


def fits_kernel(window, bwidth, vi_ref, out_ref):
    width = vi_ref.shape[1]
    vi = vi_ref[...]
    group = iota((IRREPS, width), 0)
    sizes = jnp.sum(jnp.where(vi == group, 1.0, 0.0), axis=1, keepdims=True)
    lane = iota((window, width), 1)
    irr_a = jnp.sum(
        jnp.where(lane == iota((window, width), 0), vi.astype(F32), 0.0), axis=1, keepdims=True
    )
    label = jnp.bitwise_xor(irr_a.astype(jnp.int32), vi)
    per_b = [
        jnp.sum(jnp.where(label == g, 1.0, 0.0), axis=0, keepdims=True) for g in range(IRREPS)
    ]
    per_b = jnp.concatenate(per_b, axis=0).astype(BF16)
    blocks = iota((width, LANES), 1) == lax.div(iota((width, LANES), 0), bwidth)
    members = mm(per_b, jnp.where(blocks, 1.0, 0.0).astype(BF16))
    fit = jnp.logical_and(jnp.max(sizes) <= CLASS_ROW, jnp.max(members) <= OUT_SLOTS)
    out_ref[0, 0] = jnp.where(fit, 1, 0)


def fits(window, bwidth, virt_irrep):
    flag = pl.pallas_call(
        functools.partial(fits_kernel, window, bwidth),
        out_shape=jax.ShapeDtypeStruct((1, 1), jnp.int32),
        in_specs=[pl.BlockSpec(memory_space=pltpu.VMEM)],
        out_specs=pl.BlockSpec(memory_space=pltpu.SMEM),
        name="fits",
    )(virt_irrep[None, :])
    return flag[0, 0] > 0


def table_lookup(indices, table, zero_value):
    orbital = jnp.arange(table.shape[0], dtype=jnp.int32)
    hits = indices[:, None] == orbital[None, :]
    return jnp.sum(jnp.where(hits, table[None, :], zero_value), axis=1)


def general(amplitudes, integrals, pair_occ, occ_irrep, virt_irrep, occ_energy, virt_energy):
    window_size, local_width, local_depth, full_width = integrals.shape
    integral_matrix = integrals.reshape(window_size * local_width, local_depth * full_width)
    owned_rows = pair_occ.shape[0]
    block = amplitudes.shape[0]
    blocks, owners = lax.axis_size("pair"), lax.axis_size("virt")
    here, owner = lax.axis_index("pair"), lax.axis_index("virt")

    ring = [(i, (i + 1) % blocks) for i in range(blocks)]

    def multiply(step, held, partial_value):
        rows = lax.dot_general(
            held.reshape(block, local_depth * full_width),
            integral_matrix,
            (((1,), (1,)), ((), ())),
            preferred_element_type=jnp.float32,
        )
        first = lax.rem(here - step + blocks, blocks) * block
        return lax.dynamic_update_slice_in_dim(partial_value, rows, first, 0)

    def hop(step, carry):
        held, partial_value = carry
        return lax.ppermute(held, "pair", ring), multiply(step, held, partial_value)

    empty = jnp.zeros((block * blocks, integral_matrix.shape[0]), jnp.float32)
    first_hop = hop(0, (amplitudes, empty))
    held, partial_value = lax.fori_loop(1, blocks - 1, hop, first_hop)
    partial_value = multiply(blocks - 1, held, partial_value)

    def term(step):
        first = lax.rem(owner - 1 - step + 2 * owners, owners) * owned_rows
        return lax.dynamic_slice_in_dim(partial_value, first, owned_rows, 0)

    owner_ring = [(i, (i + 1) % owners) for i in range(owners)]

    def reduce(step, total):
        return lax.ppermute(total, "virt", owner_ring) + term(step)

    ladder = lax.fori_loop(1, owners, reduce, term(0))
    ladder = ladder.reshape(owned_rows, window_size, local_width)
    b_offset = lax.axis_index("pair") * local_width
    local_sym = lax.dynamic_slice_in_dim(virt_irrep, b_offset, local_width, 0)
    local_energy = lax.dynamic_slice_in_dim(virt_energy, b_offset, local_width, 0)
    first_occ = pair_occ[:, 0]
    second_occ = pair_occ[:, 1]
    pair_sym = jnp.bitwise_xor(
        table_lookup(first_occ, occ_irrep, 0), table_lookup(second_occ, occ_irrep, 0)
    )
    pair_energy = table_lookup(first_occ, occ_energy, 0.0) + table_lookup(
        second_occ, occ_energy, 0.0
    )
    window_sym = virt_irrep[:window_size]
    total_sym = jnp.bitwise_xor(
        pair_sym[:, None, None],
        jnp.bitwise_xor(window_sym[None, :, None], local_sym[None, None, :]),
    )
    allowed = total_sym == 0
    denom = (
        pair_energy[:, None, None]
        - virt_energy[:window_size][None, :, None]
        - local_energy[None, None, :]
    )
    return jnp.where(allowed, ladder / denom, jnp.zeros_like(ladder))


def solution(mesh):
    def local(*args):
        window, bwidth = args[1].shape[:2]
        return lax.cond(
            fits(window, bwidth, args[4]), functools.partial(folded, mesh), general, *args
        )

    return jax.shard_map(
        local,
        mesh=mesh,
        in_specs=(
            P("pair", "virt", None),
            P(None, "pair", "virt", None),
            P("virt", None),
            P(),
            P(),
            P(),
            P(),
        ),
        out_specs=P("virt", None, "pair"),
        check_vma=False,
    )
```

```python
import functools

import jax
import jax.numpy as jnp
from jax import lax
from jax.experimental import pallas as pl
from jax.experimental.pallas import tpu as pltpu
from jax.sharding import PartitionSpec as P

MESH = pl.DeviceIdType.MESH
F32 = jnp.float32
BF16 = jnp.bfloat16

IRREPS = 8
LANES = 128
ROWS = (80, 96)
CHUNKS = 4
OUT_SLOTS = 64
CORES = 2


def iota(shape, dim):
    return lax.broadcasted_iota(jnp.int32, shape, dim)


def mm(a, b):
    return lax.dot_general(a, b, (((1,), (0,)), ((), ())), preferred_element_type=F32)


def split3(x):
    hi = x.astype(BF16)
    rest = x - hi.astype(F32)
    mid = rest.astype(BF16)
    return hi, mid, (rest - mid.astype(F32)).astype(BF16)


def select_dot(sel, x):
    n = x.shape[1]
    both = mm(sel, jnp.concatenate(split3(x), axis=1))
    return (both[:, 2 * n :] + both[:, n : 2 * n]) + both[:, :n]


def fold_kernel(
    chips,
    virts,
    rows_sent,
    t_hbm,
    v_hbm,
    po_ref,
    oi_ref,
    vi_ref,
    oe_ref,
    ve_ref,
    out_ref,
    t_buf,
    v_buf,
    small,
    slot_sel,
    group_sel,
    t_folded,
    t_seen,
    v_folded,
    v_mat,
    v_other,
    cls_ref,
    fold_sel,
    gathered,
    stage,
    recv,
    local_sem,
    ring_send,
    ring_recv,
    swap_send,
    swap_recv,
    piece_send,
    piece_recv,
):
    pairs, depth, width = t_buf.shape
    window, bwidth = v_buf.shape[0], v_buf.shape[1]
    abs_ = window * bwidth
    half_c = depth // 2
    chunk = half_c // CHUNKS
    class_row = rows_sent - 1

    pair = lax.axis_index("pair")
    virt = lax.axis_index("virt")
    z = lax.div(pair, CORES)
    core = lax.rem(pair, CORES)
    up = lax.rem(z + 1, chips) * CORES + core
    down = lax.rem(z + chips - 1, chips) * CORES + core
    other = z * CORES + (1 - core)
    source_core = lax.rem(lax.div(virt, 2), CORES)
    keeps_one = source_core == core
    kept = jnp.where(keeps_one, 1, 0)

    t_copy = pltpu.make_async_copy(t_hbm, t_buf, local_sem.at[0])
    v_copy = pltpu.make_async_copy(v_hbm, v_buf, local_sem.at[1])
    t_copy.start()
    v_copy.start()

    barrier = pltpu.get_barrier_semaphore()
    for q in (up, down, other):
        pl.semaphore_signal(barrier, inc=1, device_id={"pair": q}, device_id_type=MESH)

    @pl.loop(0, virts)
    def _(k):
        w = lax.rem(virt + k, virts)

        @pl.when(jnp.logical_or(w != virt, jnp.logical_not(keeps_one)))
        def _():
            pl.semaphore_signal(
                barrier,
                inc=1,
                device_id={"pair": z * CORES + source_core, "virt": w},
                device_id_type=MESH,
            )

    gathered[:, :, rows_sent:, :] = jnp.zeros((chips, half_c, LANES - rows_sent, LANES), BF16)

    vi = vi_ref[...].astype(F32)
    ve = ve_ref[...]
    lane_d = iota((width, width), 1)
    sub_d = iota((width, width), 0)
    irr_col = jnp.sum(jnp.where(lane_d == sub_d, vi, 0.0), axis=1, keepdims=True)
    lane_g = iota((width, LANES), 1)
    hot = irr_col.astype(jnp.int32) == lane_g
    hot_f = jnp.where(hot, 1.0, 0.0)
    earlier = jnp.where(lane_d < sub_d, 1.0, 0.0).astype(BF16)
    counts = mm(earlier, hot_f.astype(BF16))
    slot = jnp.sum(jnp.where(hot, counts, 0.0), axis=1, keepdims=True)
    slot_sel[...] = jnp.where(slot.astype(jnp.int32) == lane_g, 1.0, 0.0).astype(BF16)
    group_sel[...] = hot_f.astype(BF16)

    lane_c = iota((depth, width), 1)
    sub_c = iota((depth, width), 0)
    irr_c = jnp.sum(jnp.where(lane_c == virt * depth + sub_c, vi, 0.0), axis=1, keepdims=True)
    lane_s = iota((depth, LANES), 1)
    seen_class = jnp.where(
        lane_s < IRREPS, jnp.bitwise_xor(irr_c.astype(jnp.int32), lane_s), 0
    ).astype(F32)

    t_copy.wait()
    rows = pairs * depth
    t_rows = t_buf[...].reshape(rows, width)
    t_folded[...] = mm(t_rows, slot_sel[...])
    live = jnp.where(t_rows.astype(F32) != 0.0, 1.0, 0.0).astype(BF16)
    seen = mm(live, group_sel[...]).reshape(pairs, depth, LANES)
    t_seen[...] = jnp.where(seen > 0.0, seen_class[None], 0.0).reshape(rows, LANES)
    pair_cls = t_seen[pl.ds(0, pairs, stride=depth), :]
    for c in range(1, depth):
        pair_cls = jnp.maximum(pair_cls, t_seen[pl.ds(c, pairs, stride=depth), :])
    pair_cls = jnp.max(pair_cls, axis=1, keepdims=True)

    def fold_block(c2):
        x = jnp.concatenate(
            [
                t_folded[pl.ds(c2, pairs, stride=depth), :],
                t_folded[pl.ds(c2 + half_c, pairs, stride=depth), :],
            ],
            axis=0,
        )
        if c2 == 0:
            label = jnp.concatenate([pair_cls, pair_cls], axis=0)
            x = jnp.where(iota(x.shape, 1) == class_row, label, x)
        gathered[0, c2, :rows_sent, :] = jnp.transpose(x)[:rows_sent, :].astype(BF16)

    def ring_copy(way, d, ch):
        src, dst = d - 1, d
        if way == 0:
            src, dst = (chips - src) % chips, (chips - dst) % chips
        part = (pl.ds(ch * chunk, chunk), pl.ds(0, rows_sent))
        return pltpu.make_async_remote_copy(
            src_ref=gathered.at[src, part[0], part[1], :],
            dst_ref=gathered.at[dst, part[0], part[1], :],
            send_sem=ring_send.at[way, d - 1, ch],
            recv_sem=ring_recv.at[way, d - 1, ch],
            device_id={"pair": up if way == 0 else down},
            device_id_type=MESH,
        )

    far = chips // 2

    def travels(way, d, ch):
        return d < far or (d == far and ch // (CHUNKS // 2) == way)

    for c2 in range(half_c):
        fold_block(c2)
        if c2 == chunk - 1:
            pl.semaphore_wait(barrier, virts + 3 - kept)
        if (c2 + 1) % chunk == 0:
            for way in range(2):
                ring_copy(way, 1, c2 // chunk).start()

    v_copy.wait()

    @pl.loop(0, window)
    def _(a):
        v_folded[...] = mm(v_buf[a].reshape(bwidth * depth, width), slot_sel[...])
        dst = pl.ds(pl.multiple_of(a * bwidth, bwidth), bwidth)
        for c in range(depth):
            x = v_folded[pl.ds(c, bwidth, stride=depth), :].astype(BF16)
            c2 = c % half_c
            v_mat[c // half_c, dst, c2 * LANES : (c2 + 1) * LANES] = x

    swap = pltpu.make_async_remote_copy(
        src_ref=v_mat,
        dst_ref=v_other,
        send_sem=swap_send,
        recv_sem=swap_recv,
        device_id={"pair": other},
        device_id_type=MESH,
    )
    swap.start()

    lane_ab = iota((abs_, width), 1)
    sub_ab = iota((abs_, width), 0)
    sub_a = lax.div(sub_ab, bwidth)
    sub_b = sub_ab - sub_a * bwidth
    hit_a = lane_ab == sub_a
    irr_a = jnp.sum(jnp.where(hit_a, vi, 0.0), axis=1, keepdims=True).astype(jnp.int32)
    lane_k = iota((abs_, LANES), 1)
    before = jnp.where(iota((abs_, abs_), 1) < iota((abs_, abs_), 0), 1.0, 0.0).astype(BF16)
    unfold = None
    for k, q in enumerate((pair, other)):
        hit_b = lane_ab == q * bwidth + sub_b
        irr_b = jnp.sum(jnp.where(hit_b, vi, 0.0), axis=1, keepdims=True).astype(jnp.int32)
        cls = jnp.bitwise_xor(irr_a, irr_b)
        hot_ab = cls == lane_k
        hot_ab_f = jnp.where(hot_ab, 1.0, 0.0)
        ranks = jnp.where(hot_ab, mm(before, hot_ab_f.astype(BF16)), 0.0)
        rank = jnp.sum(ranks, axis=1, keepdims=True).astype(jnp.int32)
        unfold_f = jnp.where(rank == lane_k, 1.0, 0.0)
        if k == 0:
            unfold = unfold_f.astype(BF16)[:, :OUT_SLOTS]
            energy_a = jnp.sum(jnp.where(hit_a, ve, 0.0), axis=1, keepdims=True)
            energy_b = jnp.sum(jnp.where(hit_b, ve, 0.0), axis=1, keepdims=True)
        fold_sel[k] = jnp.transpose(unfold_f)[:OUT_SLOTS, :].astype(BF16)
        cls_ref[k] = jnp.broadcast_to(cls.astype(F32), (abs_, LANES))

    def piece_copy(k, index, owner):
        return pltpu.make_async_remote_copy(
            src_ref=stage.at[k, index],
            dst_ref=recv.at[virt],
            send_sem=piece_send,
            recv_sem=piece_recv,
            device_id={"pair": other if k else pair, "virt": owner},
            device_id_type=MESH,
        )

    lane = iota((1, LANES), 1)
    low = lane < pairs
    quarter = lax.div(lane, LANES // 4)

    def class_of(delta):
        tail = rows_sent - 16
        return gathered[delta, 0, tail:rows_sent, :].astype(F32)[15:16, :]

    def contract(k, deltas):
        depth_k = half_c * LANES
        blocks = [gathered[delta].reshape(depth_k, LANES) for delta in deltas]
        block = jnp.concatenate(blocks, axis=1) if len(blocks) > 1 else blocks[0]
        mat = v_other if k else v_mat
        r0 = mm(mat[0], block)
        r1 = mm(mat[1], block)
        if len(deltas) > 1:
            keep = jnp.where(low, r0[:, :LANES], r1[:, LANES:])
            move = jnp.where(low, r0[:, LANES:], r1[:, :LANES])
            row = jnp.where(low, class_of(deltas[0]), class_of(deltas[1]))
        else:
            keep, move, row = r0, r1, class_of(deltas[0])
        full = keep + pltpu.roll(move, LANES // 2, axis=1)
        full = jnp.where(cls_ref[k] == row, full, 0.0)
        folded = select_dot(fold_sel[k], full)
        per = OUT_SLOTS // 4
        for u in range(2 * len(deltas)):
            piece = jnp.zeros((per, LANES), F32)
            for q in range(4):
                x = folded[q * per : (q + 1) * per, :]
                shift = ((q - u) % 4) * (LANES // 4)
                if shift:
                    x = pltpu.roll(x, shift, axis=1)
                piece = jnp.where(quarter == q, x, piece)
            delta, half = deltas[u // 2], u % 2
            owner = (lax.rem(z + delta, chips) * CORES + core) * 2 + half
            index = delta * 2 + half
            stage[k, index] = piece
            if k:
                piece_copy(k, index, owner).start()
            else:

                @pl.when(owner != virt)
                def _():
                    piece_copy(k, index, owner).start()

                @pl.when(owner == virt)
                def _():
                    recv[virt] = piece

    def arrive(d, ch):
        for way in range(2):
            if travels(way, d, ch):
                ring_copy(way, d, ch).wait_recv()
                if travels(way, d + 1, ch):
                    ring_copy(way, d + 1, ch).start()

    todo = [(0, (0,)), (1, (0,))]
    swapped = False
    for d in range(1, far + 1):
        for ch in range(CHUNKS):
            arrive(d, ch)
            if todo:
                k, deltas = todo.pop(0)
                if k and not swapped:
                    swap.wait_recv()
                    swapped = True
                contract(k, deltas)
        deltas = (d, chips - d) if d < far else (far,)
        todo += [(0, deltas), (1, deltas)]
    for k, deltas in todo:
        contract(k, deltas)

    for held in range(2):

        @pl.when(kept == held)
        def _():
            part = recv.at[pl.ds(0, virts - held)]
            pltpu.make_async_copy(part, part, piece_recv).wait()

    total = recv[0]
    for w in range(1, virts):
        total = total + recv[w]
    shifted = [total] + [pltpu.roll(total, LANES - q * (LANES // 4), axis=1) for q in (1, 2, 3)]
    ladder = select_dot(unfold, jnp.concatenate(shifted, axis=0))

    small[...] = jnp.zeros_like(small)
    small[0:1, : oi_ref.shape[1]] = oi_ref[...].astype(F32)
    small[1:2, : oe_ref.shape[1]] = oe_ref[...]
    small[2:4, : po_ref.shape[1]] = po_ref[...].astype(F32)
    orb_irr = jnp.transpose(jnp.broadcast_to(small[0:1, :], (LANES, LANES)))
    orb_energy = jnp.transpose(jnp.broadcast_to(small[1:2, :], (LANES, LANES)))
    orb = iota((LANES, LANES), 0)
    hit_i = small[2:3, :].astype(jnp.int32) == orb
    hit_j = small[3:4, :].astype(jnp.int32) == orb
    irr_i = jnp.sum(jnp.where(hit_i, orb_irr, 0.0), axis=0, keepdims=True)
    irr_j = jnp.sum(jnp.where(hit_j, orb_irr, 0.0), axis=0, keepdims=True)
    energy_i = jnp.sum(jnp.where(hit_i, orb_energy, 0.0), axis=0, keepdims=True)
    energy_j = jnp.sum(jnp.where(hit_j, orb_energy, 0.0), axis=0, keepdims=True)
    pair_sym = jnp.bitwise_xor(irr_i.astype(jnp.int32), irr_j.astype(jnp.int32)).astype(F32)
    denom = ((energy_i + energy_j) - energy_a) - energy_b
    update = jnp.where(cls_ref[0] == pair_sym, ladder / denom, 0.0)
    update = jnp.transpose(update)[: out_ref.shape[0], :]
    for a in range(window):
        out_ref[:, a, :] = update[:, a * bwidth : (a + 1) * bwidth]

    for way in range(2):
        for d in range(1, far + 1):
            for ch in range(CHUNKS):
                if travels(way, d, ch):
                    ring_copy(way, d, ch).wait_send()
    swap.wait_send()
    for held in range(2):

        @pl.when(kept == held)
        def _():
            part = recv.at[pl.ds(0, virts - held)]
            pltpu.make_async_copy(part, part, piece_send).wait()


def folded(
    mesh,
    rows_sent,
    amplitudes,
    integrals,
    pair_occ,
    occ_irrep,
    virt_irrep,
    occ_energy,
    virt_energy,
):
    chips, virts = mesh.shape["pair"] // CORES, mesh.shape["virt"]
    pairs, depth, width = amplitudes.shape
    window, bwidth = integrals.shape[:2]
    abs_ = window * bwidth
    owned = pair_occ.shape[0]
    half_c = depth // 2
    per = OUT_SLOTS // 4
    vmem = pl.BlockSpec(memory_space=pltpu.VMEM)
    hbm = pl.BlockSpec(memory_space=pl.ANY)
    dma = pltpu.SemaphoreType.DMA
    return pl.pallas_call(
        functools.partial(fold_kernel, chips, virts, rows_sent),
        out_shape=jax.ShapeDtypeStruct((owned, window, bwidth), F32),
        in_specs=[hbm, hbm] + [vmem] * 5,
        out_specs=vmem,
        scratch_shapes=[
            pltpu.VMEM(amplitudes.shape, BF16),
            pltpu.VMEM(integrals.shape, BF16),
            pltpu.VMEM((8, LANES), F32),
            pltpu.VMEM((width, LANES), BF16),
            pltpu.VMEM((width, LANES), BF16),
            pltpu.VMEM((pairs * depth, LANES), F32),
            pltpu.VMEM((pairs * depth, LANES), F32),
            pltpu.VMEM((bwidth * depth, LANES), F32),
            pltpu.VMEM((2, abs_, half_c * LANES), BF16),
            pltpu.VMEM((2, abs_, half_c * LANES), BF16),
            pltpu.VMEM((2, abs_, LANES), F32),
            pltpu.VMEM((2, OUT_SLOTS, abs_), BF16),
            pltpu.VMEM((chips, half_c, LANES, LANES), BF16),
            pltpu.VMEM((2, 2 * chips, per, LANES), F32),
            pltpu.VMEM((virts, per, LANES), F32),
            dma((2,)),
            dma((2, chips // 2, CHUNKS)),
            dma((2, chips // 2, CHUNKS)),
            dma,
            dma,
            dma,
            dma,
        ],
        compiler_params=pltpu.CompilerParams(collective_id=rows_sent, has_side_effects=True),
        name=f"ladder_fold_{rows_sent}",
    )(
        amplitudes,
        integrals,
        pair_occ.T,
        occ_irrep[None, :],
        virt_irrep[None, :],
        occ_energy[None, :],
        virt_energy[None, :],
    )


def fits_kernel(window, bwidth, vi_ref, out_ref):
    width = vi_ref.shape[1]
    vi = vi_ref[...]
    group = iota((IRREPS, width), 0)
    sizes = jnp.sum(jnp.where(vi == group, 1.0, 0.0), axis=1, keepdims=True)
    lane = iota((window, width), 1)
    irr_a = jnp.sum(
        jnp.where(lane == iota((window, width), 0), vi.astype(F32), 0.0), axis=1, keepdims=True
    )
    label = jnp.bitwise_xor(irr_a.astype(jnp.int32), vi)
    per_b = [
        jnp.sum(jnp.where(label == g, 1.0, 0.0), axis=0, keepdims=True) for g in range(IRREPS)
    ]
    per_b = jnp.concatenate(per_b, axis=0).astype(BF16)
    blocks = iota((width, LANES), 1) == lax.div(iota((width, LANES), 0), bwidth)
    members = mm(per_b, jnp.where(blocks, 1.0, 0.0).astype(BF16))
    largest = jnp.max(sizes)
    case = 0
    for rows in ROWS:
        case += jnp.where(largest <= rows - 1, 0, 1)
    out_ref[0, 0] = jnp.where(jnp.max(members) <= OUT_SLOTS, case, len(ROWS))


def fits(window, bwidth, virt_irrep):
    case = pl.pallas_call(
        functools.partial(fits_kernel, window, bwidth),
        out_shape=jax.ShapeDtypeStruct((1, 1), jnp.int32),
        in_specs=[pl.BlockSpec(memory_space=pltpu.VMEM)],
        out_specs=pl.BlockSpec(memory_space=pltpu.SMEM),
        name="fits",
    )(virt_irrep[None, :])
    return case[0, 0]


def table_lookup(indices, table, zero_value):
    orbital = jnp.arange(table.shape[0], dtype=jnp.int32)
    hits = indices[:, None] == orbital[None, :]
    return jnp.sum(jnp.where(hits, table[None, :], zero_value), axis=1)


def general(amplitudes, integrals, pair_occ, occ_irrep, virt_irrep, occ_energy, virt_energy):
    window_size, local_width, local_depth, full_width = integrals.shape
    integral_matrix = integrals.reshape(window_size * local_width, local_depth * full_width)
    owned_rows = pair_occ.shape[0]
    block = amplitudes.shape[0]
    blocks, owners = lax.axis_size("pair"), lax.axis_size("virt")
    here, owner = lax.axis_index("pair"), lax.axis_index("virt")

    ring = [(i, (i + 1) % blocks) for i in range(blocks)]

    def multiply(step, held, partial_value):
        rows = lax.dot_general(
            held.reshape(block, local_depth * full_width),
            integral_matrix,
            (((1,), (1,)), ((), ())),
            preferred_element_type=jnp.float32,
        )
        first = lax.rem(here - step + blocks, blocks) * block
        return lax.dynamic_update_slice_in_dim(partial_value, rows, first, 0)

    def hop(step, carry):
        held, partial_value = carry
        return lax.ppermute(held, "pair", ring), multiply(step, held, partial_value)

    empty = jnp.zeros((block * blocks, integral_matrix.shape[0]), jnp.float32)
    first_hop = hop(0, (amplitudes, empty))
    held, partial_value = lax.fori_loop(1, blocks - 1, hop, first_hop)
    partial_value = multiply(blocks - 1, held, partial_value)

    def term(step):
        first = lax.rem(owner - 1 - step + 2 * owners, owners) * owned_rows
        return lax.dynamic_slice_in_dim(partial_value, first, owned_rows, 0)

    owner_ring = [(i, (i + 1) % owners) for i in range(owners)]

    def reduce(step, total):
        return lax.ppermute(total, "virt", owner_ring) + term(step)

    ladder = lax.fori_loop(1, owners, reduce, term(0))
    ladder = ladder.reshape(owned_rows, window_size, local_width)
    b_offset = lax.axis_index("pair") * local_width
    local_sym = lax.dynamic_slice_in_dim(virt_irrep, b_offset, local_width, 0)
    local_energy = lax.dynamic_slice_in_dim(virt_energy, b_offset, local_width, 0)
    first_occ = pair_occ[:, 0]
    second_occ = pair_occ[:, 1]
    pair_sym = jnp.bitwise_xor(
        table_lookup(first_occ, occ_irrep, 0), table_lookup(second_occ, occ_irrep, 0)
    )
    pair_energy = table_lookup(first_occ, occ_energy, 0.0) + table_lookup(
        second_occ, occ_energy, 0.0
    )
    window_sym = virt_irrep[:window_size]
    total_sym = jnp.bitwise_xor(
        pair_sym[:, None, None],
        jnp.bitwise_xor(window_sym[None, :, None], local_sym[None, None, :]),
    )
    allowed = total_sym == 0
    denom = (
        pair_energy[:, None, None]
        - virt_energy[:window_size][None, :, None]
        - local_energy[None, None, :]
    )
    return jnp.where(allowed, ladder / denom, jnp.zeros_like(ladder))


def solution(mesh):
    def local(*args):
        window, bwidth = args[1].shape[:2]
        branches = [functools.partial(folded, mesh, rows) for rows in ROWS] + [general]
        return lax.switch(fits(window, bwidth, args[4]), branches, *args)

    return jax.shard_map(
        local,
        mesh=mesh,
        in_specs=(
            P("pair", "virt", None),
            P(None, "pair", "virt", None),
            P("virt", None),
            P(),
            P(),
            P(),
            P(),
        ),
        out_specs=P("virt", None, "pair"),
        check_vma=False,
    )
```
